32 devices in a mesh: rows: 8 (over z, x), narrow: 4 (over y, core).
Axes of the slice: x: 2, y: 2, z: 4, core: 2. Of those that a mesh axis runs over, the one named last changes fastest.
Arguments:
- hidden_in: bfloat16 [1024, 8, 768], P('narrow', 'rows'), may hold values from -6 to 6
- memory: bfloat16 [4096, 8, 768], P('narrow', 'rows'), may hold values from -6 to 6
- cotangent: bfloat16 [1024, 8, 768], P('narrow', 'rows'), may hold values from -6 to 6
- seg_ids: int32 [8, 1024], P('rows'), may hold values from 0 to 7, never falling along the last dimension, each value on 1 to 256 neighbouring positions
- mem_lengths: int32 [8, 8], P('rows'), may hold values from 1 to 1024, 4096 in all within a row
- norm_self: float32 [768], replicated, may hold values from 0.25 to 1.75
- norm_cross: float32 [768], replicated, may hold values from 0.25 to 1.75
- norm_ffn: float32 [768], replicated, may hold values from 0.25 to 1.75
- bias_table: float32 [32, 12], P(None, 'narrow'), may hold values from -4 to 4
- self_query: bfloat16 [768, 768], P(None, 'narrow'), may hold values from -0.0546875 to 0.0546875
- self_key: bfloat16 [768, 768], P(None, 'narrow'), may hold values from -0.21875 to 0.21875
- self_value: bfloat16 [768, 768], P(None, 'narrow'), may hold values from -0.21875 to 0.21875
- self_out: bfloat16 [768, 768], P('narrow'), may hold values from -0.625 to 0.625
- cross_query: bfloat16 [768, 768], P(None, 'narrow'), may hold values from -0.0546875 to 0.0546875
- cross_key: bfloat16 [768, 768], P(None, 'narrow'), may hold values from -0.21875 to 0.21875
- cross_value: bfloat16 [768, 768], P(None, 'narrow'), may hold values from -0.21875 to 0.21875
- cross_out: bfloat16 [768, 768], P('narrow'), may hold values from -0.875 to 0.875
- ffn_gate: bfloat16 [768, 2048], P(None, 'narrow'), may hold values from -0.21875 to 0.21875
- ffn_up: bfloat16 [768, 2048], P(None, 'narrow'), may hold values from -0.21875 to 0.21875
- ffn_down: bfloat16 [2048, 768], P('narrow'), may hold values from -0.125 to 0.125
Outputs:
- layer_out: bfloat16 [1024, 8, 768], P('narrow', 'rows')
- grad_input: float32 [1024, 8, 768], P('narrow', 'rows')
- grad_memory: float32 [4096, 8, 768], P('narrow', 'rows')
- grad_norm_self: float32 [768], replicated
- grad_norm_cross: float32 [768], replicated
- grad_norm_ffn: float32 [768], replicated
- grad_bias_table: float32 [32, 12], P(None, 'narrow')
- grad_self_query: float32 [768, 768], P(None, 'narrow')
- grad_self_key: float32 [768, 768], P(None, 'narrow')
- grad_self_value: float32 [768, 768], P(None, 'narrow')
- grad_self_out: float32 [768, 768], P('narrow')
- grad_cross_query: float32 [768, 768], P(None, 'narrow')
- grad_cross_key: float32 [768, 768], P(None, 'narrow')
- grad_cross_value: float32 [768, 768], P(None, 'narrow')
- grad_cross_out: float32 [768, 768], P('narrow')
- grad_ffn_gate: float32 [768, 2048], P(None, 'narrow')
- grad_ffn_up: float32 [768, 2048], P(None, 'narrow')
- grad_ffn_down: float32 [2048, 768], P('narrow')
The draws below stay inside these ranges and needn't reach their ends.
Inputs may be any that keep to these rules, and one draw needn't show every extreme that they name: `seg_ids`: along a row the group ids never fall; a group holds at most 256 positions. `mem_lengths`: A row's lengths sum to 4096; group g's memory follows those of the groups before it.
All inputs are finite; a program needn't handle non-finite values.
Results may differ from the reference program's by a relative error of at most 0.025.
The reference program's roundings to bfloat16 on the way count: a program that leaves them out, or rounds other values in their place, can miss the bound.
Values may be sent and summed in bfloat16 or wider, within the bound.
No kernel may reach another device: no remote copies, remote signals or barrier semaphores. Data moves between devices by JAX's collectives and lax.ppermute only.
A program may use at most 320 MiB of HBM per device.

```python
import math
import jax
import jax.numpy as jnp
import numpy as np
from jax import lax

D = 768
HEADS = 12
HEAD_DIM = 64
FF = 2048
NUM_BUCKETS = 32
LEN = 1024
MEM = 4096
GROUPS = 8
SEG_MOST = 256
MEM_MOST = 1024
QBLOCK = 512
SEQS = 8


def levels(rng, dims, split, least, top_value):
    def one(axis_at, blocks):
        draws = jax.random.uniform(jax.random.fold_in(jax.random.fold_in(rng, 6), axis_at), (blocks,), jnp.float32, least / len(split), top_value / len(split))
        return jnp.repeat(jnp.exp(draws), dims[axis_at] // blocks).reshape((-1,) + (1,) * (len(dims) - axis_at - 1))

    loudness = one(*split[0])
    for cut in split[1:]:
        loudness = loudness * one(*cut)
    return loudness


def profile(count, total, most, slope):
    portions = [(1 << 20) // math.isqrt(grade ** slope) + 1 for grade in range(2, count + 1)]
    rest, counts = total - most - (count - 1), [1] * (count - 1)
    while rest > 0:
        free = [i for i in range(count - 1) if counts[i] < most]
        pool, remaining = sum([portions[i] for i in free]), rest
        for i in free:
            addition = min(most - counts[i], max(1, remaining * portions[i] // pool), rest)
            counts[i] = counts[i] + addition
            rest = rest - addition
    return np.array([most] + counts)


def uneven(own_key, count, total, reach, skew):
    if count == 2:
        one = jax.random.randint(own_key, (), max(1, total - reach), min(reach, total - 1) + 1)
        return jnp.stack([one, total - one])
    tallies = jnp.asarray(profile(count, total, reach, skew), jnp.int32)
    pairs = (count - 1) // 2
    giver, sink = tallies[1:1 + 2 * pairs:2], tallies[2:2 + 2 * pairs:2]
    room = jnp.minimum(giver - 1, reach - sink)
    shifted = jax.random.randint(jax.random.fold_in(own_key, 1), (pairs,), 0, 1 << 20) % (room + 1)
    tallies = tallies.at[1:1 + 2 * pairs:2].set(giver - shifted).at[2:2 + 2 * pairs:2].set(sink + shifted)
    return tallies[jax.random.permutation(jax.random.fold_in(own_key, 2), count)]


def noise(stream_key, shape, width, most, split=(), kind=jnp.bfloat16):
    array = width * jax.random.normal(stream_key, shape, jnp.float32)
    if split:
        array = array * levels(stream_key, shape, split, -0.22, 0.18)
    return jnp.clip(array, -most, most).astype(kind)


def setup_inputs(seed: int = 0) -> dict:
    streams_of = jax.random.split(jax.random.key(seed), 21)
    return {
        "hidden_in": noise(streams_of[0], (LEN, SEQS, D), 1.0, 6.0, ((0, 4), (1, 8))),
        "memory": noise(streams_of[1], (MEM, SEQS, D), 1.0, 6.0, ((0, 4), (1, 8))),
        "cotangent": noise(streams_of[2], (LEN, SEQS, D), 1.0, 6.0, ((0, 4), (1, 8))),
        "seg_ids": jax.vmap(lambda own: jnp.searchsorted(jnp.cumsum(uneven(own, GROUPS, LEN, SEG_MOST, 1)), jnp.arange(LEN), side="right"))(jax.random.split(streams_of[3], SEQS)).reshape((SEQS, LEN)).astype(jnp.int32),
        "mem_lengths": jax.vmap(lambda own: uneven(own, GROUPS, MEM, MEM_MOST, 1))(jax.random.split(streams_of[4], SEQS)).reshape((SEQS, GROUPS)).astype(jnp.int32),
        "norm_self": jnp.clip(1.0 + 0.15 * jax.random.normal(streams_of[5], (D,), jnp.float32), 0.25, 1.75),
        "norm_cross": jnp.clip(1.0 + 0.15 * jax.random.normal(streams_of[6], (D,), jnp.float32), 0.25, 1.75),
        "norm_ffn": jnp.clip(1.0 + 0.15 * jax.random.normal(streams_of[7], (D,), jnp.float32), 0.25, 1.75),
        "bias_table": noise(streams_of[8], (NUM_BUCKETS, HEADS), 1.0, 4.0, ((1, 4),), jnp.float32),
        "self_query": noise(streams_of[9], (D, HEADS * HEAD_DIM), (16 * D) ** -0.5, 0.0546875, ((1, 4),)),
        "self_key": noise(streams_of[10], (D, HEADS * HEAD_DIM), D ** -0.5, 0.21875, ((1, 4),)),
        "self_value": noise(streams_of[11], (D, HEADS * HEAD_DIM), D ** -0.5, 0.21875, ((1, 4),)),
        "self_out": noise(streams_of[12], (HEADS * HEAD_DIM, D), (D // 8) ** -0.5, 0.625, ((0, 4),)),
        "cross_query": noise(streams_of[13], (D, HEADS * HEAD_DIM), (16 * D) ** -0.5, 0.0546875, ((1, 4),)),
        "cross_key": noise(streams_of[14], (D, HEADS * HEAD_DIM), D ** -0.5, 0.21875, ((1, 4),)),
        "cross_value": noise(streams_of[15], (D, HEADS * HEAD_DIM), D ** -0.5, 0.21875, ((1, 4),)),
        "cross_out": noise(streams_of[16], (HEADS * HEAD_DIM, D), (D // 16) ** -0.5, 0.875, ((0, 4),)),
        "ffn_gate": noise(streams_of[17], (D, FF), D ** -0.5, 0.21875, ((1, 4),)),
        "ffn_up": noise(streams_of[18], (D, FF), D ** -0.5, 0.21875, ((1, 4),)),
        "ffn_down": noise(streams_of[19], (FF, D), FF ** -0.5, 0.125, ((0, 4),)),
    }


precise = lax.Precision.HIGHEST
masked_score = -1e+30
epsilon = 1e-06
bucket_edges = np.ceil(16.0 * 8.0 ** (np.arange(1, 16) / 16.0)).astype(np.int32)

@jax.custom_vjp
def low(v):
    return lax.optimization_barrier(v.astype(jnp.bfloat16)).astype(jnp.float32)

@jax.custom_vjp
def low_back(v):
    return v

def low_keep(v):
    return (low(v), None)

def low_pass(kept, grad):
    return (grad,)

def back_keep(v):
    return (v, None)

def back_low(kept, grad):
    return (low(grad),)
low.defvjp(low_keep, low_pass)
low_back.defvjp(back_keep, back_low)

def bucket_of(distance):
    nearby = jnp.maximum(distance, 0)
    distant = 16 + lax.optimization_barrier(jnp.sum((nearby[..., None] >= jnp.asarray(bucket_edges)).astype(jnp.int32), axis=-1))
    return jnp.where(nearby < 16, nearby, distant).astype(jnp.int32)

def rms(values, norm_gain):
    return values * lax.rsqrt(lax.optimization_barrier(jnp.mean(values * values, axis=-1, keepdims=True)) + epsilon) * norm_gain

def product(left, right):
    return jnp.dot(left, right, precision=precise)

def attend(row_block, keys_seq, values_seq, bias_full, allowed):
    scores_raw = jnp.einsum('qhe,khe->hqk', row_block, keys_seq, precision=precise) + bias_full
    scores = jnp.where(allowed[None], low_back(scores_raw), masked_score)
    weights = jax.nn.softmax(scores, axis=-1)
    return jnp.einsum('hqk,khe->qhe', low(weights), values_seq, precision=precise)

def layer_one(params, tokens, memory_rows, segment_row, memory_lengths):
    table, gain_self, gain_cross, gain_ffn, w_query, w_key, w_value, w_out, c_query, c_key, c_value, c_out, w_gate, w_up, w_down = params
    positions = jnp.arange(LEN, dtype=jnp.int32)
    starts = (jnp.arange(LEN // QBLOCK, dtype=jnp.int32) * QBLOCK).astype(jnp.int32)
    normed_a = low(rms(tokens, gain_self))
    query_a = low_back(low(product(normed_a, w_query))).reshape(LEN, HEADS, HEAD_DIM)
    key_a = low_back(low(product(normed_a, w_key))).reshape(LEN, HEADS, HEAD_DIM)
    value_a = low_back(low(product(normed_a, w_value))).reshape(LEN, HEADS, HEAD_DIM)

    def self_block(offset):
        row_block = lax.dynamic_slice_in_dim(query_a, offset, QBLOCK, 0)
        query_pos = offset + jnp.arange(QBLOCK, dtype=jnp.int32)
        distance = (query_pos[:, None] - positions[None, :]).astype(jnp.int32)
        bias_full = jnp.transpose(table[bucket_of(distance)], (2, 0, 1))
        segment_rows = lax.dynamic_slice_in_dim(segment_row, offset, QBLOCK, 0)
        allowed = (distance >= 0) & (segment_rows[:, None] == segment_row[None, :])
        return attend(row_block, key_a, value_a, bias_full, allowed)
    out_a = lax.map(jax.checkpoint(self_block), starts).reshape(LEN, HEADS * HEAD_DIM)
    first_h = tokens + low_back(product(low_back(low(out_a)), w_out))
    normed_b = low(rms(first_h, gain_cross))
    query_b = low_back(low(product(normed_b, c_query))).reshape(LEN, HEADS, HEAD_DIM)
    key_b = low_back(low(product(memory_rows, c_key))).reshape(MEM, HEADS, HEAD_DIM)
    value_b = low_back(low(product(memory_rows, c_value))).reshape(MEM, HEADS, HEAD_DIM)
    group_ends = jnp.cumsum(memory_lengths).astype(jnp.int32)
    mem_positions = jnp.arange(MEM, dtype=jnp.int32)
    memory_group = lax.optimization_barrier(jnp.sum((mem_positions[:, None] >= group_ends[None, :]).astype(jnp.int32), axis=1)).astype(jnp.int32)

    def cross_block(offset):
        row_block = lax.dynamic_slice_in_dim(query_b, offset, QBLOCK, 0)
        segment_rows = lax.dynamic_slice_in_dim(segment_row, offset, QBLOCK, 0)
        allowed = segment_rows[:, None] == memory_group[None, :]
        return attend(row_block, key_b, value_b, 0.0, allowed)
    out_b = lax.map(jax.checkpoint(cross_block), starts).reshape(LEN, HEADS * HEAD_DIM)
    second_h = first_h + low_back(product(low_back(low(out_b)), c_out))
    normed_c = low(rms(second_h, gain_ffn))
    gate = low_back(product(normed_c, w_gate))
    up_proj = low_back(product(normed_c, w_up))
    hidden = low(jax.nn.gelu(gate, approximate=True) * up_proj)
    return second_h + low_back(product(hidden, w_down))

def forward(params, hidden_f, memory_f, seg_ids, mem_lengths):

    def one_sequence(items):
        return layer_one(params, items[0], items[1], items[2], items[3])
    outputs = lax.map(jax.checkpoint(one_sequence), (jnp.swapaxes(hidden_f, 0, 1), jnp.swapaxes(memory_f, 0, 1), seg_ids, mem_lengths))
    return jnp.swapaxes(outputs, 0, 1)

def reference(hidden_in, memory, cotangent, seg_ids, mem_lengths, norm_self, norm_cross, norm_ffn, bias_table, self_query, self_key, self_value, self_out, cross_query, cross_key, cross_value, cross_out, ffn_gate, ffn_up, ffn_down):
    params = tuple((weight.astype(jnp.float32) for weight in (bias_table, norm_self, norm_cross, norm_ffn, self_query, self_key, self_value, self_out, cross_query, cross_key, cross_value, cross_out, ffn_gate, ffn_up, ffn_down)))
    hidden_f = hidden_in.astype(jnp.float32)
    memory_f = memory.astype(jnp.float32)

    def wrapped(params_in, hidden_arg, memory_arg):
        return forward(params_in, hidden_arg, memory_arg, seg_ids, mem_lengths)
    layer_f, back_fn = jax.vjp(wrapped, params, hidden_f, memory_f)
    grad_params, grad_input, grad_memory = back_fn(cotangent.astype(jnp.float32))
    return (layer_f.astype(jnp.bfloat16), grad_input, grad_memory, grad_params[1], grad_params[2], grad_params[3], grad_params[0], grad_params[4], grad_params[5], grad_params[6], grad_params[7], grad_params[8], grad_params[9], grad_params[10], grad_params[11], grad_params[12], grad_params[13], grad_params[14])
```

```python
import functools
import math

import jax
import jax.numpy as jnp
import numpy as np
from jax import lax
from jax.experimental import pallas as pl
from jax.experimental.pallas import tpu as pltpu
from jax.sharding import PartitionSpec as P

f32 = jnp.float32
bf16 = jnp.bfloat16
masked_score = -1e30
epsilon = 1e-06
bucket_edges = [int(v) for v in np.ceil(16.0 * 8.0 ** (np.arange(1, 16) / 16.0))]
bucket_starts = list(range(17)) + bucket_edges

QB = 128
KT = 256
MB = 512
BAND = 256
WIDE = BAND + QB


def mm(left, right):
    return lax.dot_general(left, right, (((1,), (0,)), ((), ())), preferred_element_type=f32)


def mm_nt(left, right):
    return lax.dot_general(left, right, (((1,), (1,)), ((), ())), preferred_element_type=f32)


def mm_tn(left, right):
    return lax.dot_general(left, right, (((0,), (0,)), ((), ())), preferred_element_type=f32)


def vmem(count):
    return [pl.BlockSpec(memory_space=pltpu.VMEM)] * count


def smem(count):
    return [pl.BlockSpec(memory_space=pltpu.SMEM)] * count


def shape(dims, kind):
    return jax.ShapeDtypeStruct(dims, kind)


def run(kernel, name, scalars, arrays, outs, scratch=(), flops=0, moved=0):
    return pl.pallas_call(
        kernel,
        name=name,
        in_specs=smem(len(scalars)) + vmem(len(arrays)),
        out_specs=vmem(len(outs)),
        out_shape=list(outs),
        scratch_shapes=list(scratch),
        compiler_params=pltpu.CompilerParams(vmem_limit_bytes=60 * 1024 * 1024),
        cost_estimate=pl.CostEstimate(
            flops=int(flops), bytes_accessed=int(moved), transcendentals=0
        ),
    )(*scalars, *arrays)


def head_masks(rows, width, heads):
    lane = lax.broadcasted_iota(jnp.int32, (rows, width), 1)
    size = width // heads
    return [(lane >= h * size) & (lane < (h + 1) * size) for h in range(heads)]


def rms_scale(values):
    return lax.rsqrt(jnp.mean(values * values, axis=-1, keepdims=True) + epsilon)


def band_distance():
    row = lax.broadcasted_iota(jnp.int32, (WIDE, QB), 0)
    lane = lax.broadcasted_iota(jnp.int32, (WIDE, QB), 1)
    return lane + BAND - row


def bias_kernel(heads, table, out):
    distance = band_distance()
    values = [jnp.full((WIDE, QB), table[0, h], f32) for h in range(heads)]
    for bucket in range(1, len(bucket_starts)):
        reached = distance >= bucket_starts[bucket]
        values = [jnp.where(reached, table[bucket, h], values[h]) for h in range(heads)]
    for h in range(heads):
        out[:, h * QB : (h + 1) * QB] = jnp.where(distance >= 0, values[h], masked_score)


def bias_grad_kernel(heads, grads, out):
    distance = band_distance()
    count = len(bucket_starts)
    for bucket in range(count):
        inside = distance >= bucket_starts[bucket]
        if bucket + 1 < count:
            inside = inside & (distance < bucket_starts[bucket + 1])
        for h in range(heads):
            out[h, bucket : bucket + 1, :] = jnp.sum(
                jnp.where(inside, grads[:, h * QB : (h + 1) * QB], 0.0), axis=0, keepdims=True
            )


def fill_masked(target, place, values, masks):
    for h, mask in enumerate(masks):
        target[h, pl.ds(place, values.shape[0]), :] = jnp.where(mask, values, 0.0).astype(bf16)


def stacked(masked, cols):
    return jnp.concatenate([masked[h, cols, :] for h in range(masked.shape[0])], axis=0)


def thrice(row, count):
    return jnp.concatenate([row] * count, axis=1)


def head_rows(ref, cols):
    return jnp.concatenate([ref[h : h + 1, cols] for h in range(3)], axis=1)


def self_forward_kernel(
    heads,
    index,
    starts,
    bias,
    a0,
    a1,
    a2,
    a3,
    w_query,
    w_key,
    w_value,
    w_key_t,
    w_value_t,
    q_masked,
    k_out,
    v_out,
    kt_out,
    ot_out,
    lse_out,
    o_full,
    o0,
    o1,
    o2,
    o3,
    vt,
):
    me = index[0]
    rows, width = a0.shape[0], w_query.shape[1]
    size = width // heads
    masks = head_masks(rows, width, heads)
    for rel, part in enumerate((a0, a1, a2, a3)):
        place = pl.multiple_of((me ^ rel) * rows, rows)
        values = part[...]
        fill_masked(q_masked, place, mm(values, w_query[...]), masks)
        k_out[pl.ds(place, rows), :] = mm(values, w_key[...]).astype(bf16)
        v_out[pl.ds(place, rows), :] = mm(values, w_value[...]).astype(bf16)
        kt_out[:, pl.ds(place, rows)] = mm_nt(w_key_t[...], values).astype(bf16)
        vt[:, pl.ds(place, rows)] = mm_nt(w_value_t[...], values).astype(bf16)
    length = k_out.shape[0]
    for block in range(length // QB):
        low = max(0, block * QB - BAND)
        span = (block + 1) * QB - low
        cols = slice(block * QB, (block + 1) * QB)
        keys = k_out[low : low + span, :]
        begin = thrice(starts[:, cols], heads)
        allowed = lax.broadcasted_iota(jnp.int32, (span, heads * QB), 0) + low >= begin
        scores = mm_nt(keys, stacked(q_masked, cols)) + bias[WIDE - span :, :]
        scores = jnp.where(allowed, scores, masked_score)
        highest = jnp.max(scores, axis=0, keepdims=True)
        exponent = jnp.exp(scores - highest)
        total = jnp.sum(exponent, axis=0, keepdims=True)
        weights = (exponent * (1.0 / total)).astype(bf16)
        logsum = highest + jnp.log(total)
        for h in range(heads):
            part = slice(h * size, (h + 1) * size)
            at = slice(h * QB, (h + 1) * QB)
            ot_out[part, cols] = mm(vt[part, low : low + span], weights[:, at])
            lse_out[h : h + 1, cols] = logsum[:, at]
    for rel, piece in enumerate((o0, o1, o2, o3)):
        place = pl.multiple_of((me ^ rel) * rows, rows)
        piece[...] = ot_out[:, pl.ds(place, rows)].astype(bf16)
        o_full[:, rel * rows : (rel + 1) * rows] = piece[...]


def self_backward_kernel(
    heads,
    index,
    starts,
    bias,
    g0,
    g1,
    g2,
    g3,
    w_out,
    q_masked,
    keys_ref,
    values_ref,
    kt_ref,
    ot_ref,
    lse_ref,
    d_full,
    p0,
    p1,
    p2,
    p3,
    bias_out,
    do_masked,
    do_t,
    dq_t,
    dk_acc,
    dv_acc,
):
    me = index[0]
    rows, width = g0.shape[0], w_out.shape[0]
    size = width // heads
    masks = head_masks(rows, width, heads)
    for rel, part in enumerate((g0, g1, g2, g3)):
        place = pl.multiple_of((me ^ rel) * rows, rows)
        values = part[...]
        fill_masked(do_masked, place, mm_nt(values, w_out[...]), masks)
        do_t[:, pl.ds(place, rows)] = mm_nt(w_out[...], values).astype(bf16).astype(f32)
    bias_out[...] = jnp.zeros_like(bias_out)
    dk_acc[...] = jnp.zeros_like(dk_acc)
    dv_acc[...] = jnp.zeros_like(dv_acc)
    length = keys_ref.shape[0]
    for block in range(length // QB):
        low = max(0, block * QB - BAND)
        span = (block + 1) * QB - low
        cols = slice(block * QB, (block + 1) * QB)
        keys = keys_ref[low : low + span, :]
        values = values_ref[low : low + span, :]
        begin = thrice(starts[:, cols], heads)
        allowed = lax.broadcasted_iota(jnp.int32, (span, heads * QB), 0) + low >= begin
        stacked_q = stacked(q_masked, cols)
        stacked_o = stacked(do_masked, cols)
        scores = mm_nt(keys, stacked_q) + bias[WIDE - span :, :] - head_rows(lse_ref, cols)
        weights = jnp.exp(jnp.where(allowed, scores, masked_score))
        inner = do_t[:, cols] * ot_ref[:, cols]
        inner = jnp.concatenate(
            [
                jnp.sum(inner[h * size : (h + 1) * size], axis=0, keepdims=True)
                for h in range(heads)
            ],
            axis=1,
        )
        grads = (weights * (mm_nt(values, stacked_o) - inner)).astype(bf16)
        bias_out[WIDE - span :, :] += grads.astype(f32)
        for h in range(heads):
            part = slice(h * size, (h + 1) * size)
            dq_t[part, cols] = mm(
                kt_ref[part, low : low + span], grads[:, h * QB : (h + 1) * QB]
            ).astype(bf16)
        dk_acc[low : low + span, :] += mm(grads, stacked_q)
        dv_acc[low : low + span, :] += mm(weights.astype(bf16), stacked_o)
    for rel, piece in enumerate((p0, p1, p2, p3)):
        place = pl.multiple_of((me ^ rel) * rows, rows)
        piece[0] = dq_t[:, pl.ds(place, rows)]
        piece[1] = dk_acc[pl.ds(place, rows), :].T.astype(bf16)
        piece[2] = dv_acc[pl.ds(place, rows), :].T.astype(bf16)
        for n in range(3):
            d_full[n * width : (n + 1) * width, rel * rows : (rel + 1) * rows] = piece[n]


def memory_kernel(x, w_key, w_value, w_key_t, w_value_t, k_out, v_out, kt_out, vt_out):
    values = x[...]
    k_out[...] = mm(values, w_key[...]).astype(bf16)
    v_out[...] = mm(values, w_value[...]).astype(bf16)
    kt_out[...] = mm_nt(w_key_t[...], values).astype(bf16)
    vt_out[...] = mm_nt(w_value_t[...], values).astype(bf16)


def project_memory(memory_all, w_key, w_value, w_key_t, w_value_t):
    count, width = memory_all.shape
    local = w_key.shape[1]
    return pl.pallas_call(
        memory_kernel,
        name="project_memory",
        grid=(count // MB,),
        in_specs=[
            pl.BlockSpec((MB, width), lambda i: (i, 0)),
            pl.BlockSpec((width, local), lambda i: (0, 0)),
            pl.BlockSpec((width, local), lambda i: (0, 0)),
            pl.BlockSpec((local, width), lambda i: (0, 0)),
            pl.BlockSpec((local, width), lambda i: (0, 0)),
        ],
        out_specs=[
            pl.BlockSpec((MB, local), lambda i: (i, 0)),
            pl.BlockSpec((MB, local), lambda i: (i, 0)),
            pl.BlockSpec((local, MB), lambda i: (0, i)),
            pl.BlockSpec((local, MB), lambda i: (0, i)),
        ],
        out_shape=[
            shape((count, local), bf16),
            shape((count, local), bf16),
            shape((local, count), bf16),
            shape((local, count), bf16),
        ],
        cost_estimate=pl.CostEstimate(
            flops=8 * count * width * local, bytes_accessed=2 * count * (width + 4 * local),
            transcendentals=0,
        ),
    )(memory_all, w_key, w_value, w_key_t, w_value_t)


def cross_forward_kernel(
    heads,
    index,
    first_tile,
    tile_count,
    lows,
    highs,
    b0,
    b1,
    b2,
    b3,
    w_query,
    keys_ref,
    vt_ref,
    q_masked,
    ot_out,
    lse_out,
    o_full,
    o0,
    o1,
    o2,
    o3,
):
    me = index[0]
    rows, width = b0.shape[0], w_query.shape[1]
    size = width // heads
    wide = heads * QB
    masks = head_masks(rows, width, heads)
    for rel, part in enumerate((b0, b1, b2, b3)):
        place = pl.multiple_of((me ^ rel) * rows, rows)
        fill_masked(q_masked, place, mm(part[...], w_query[...]), masks)
    length = q_masked.shape[1]
    key_row = lax.broadcasted_iota(jnp.int32, (KT, wide), 0)

    def block_step(block, unused):
        column = pl.multiple_of(block * QB, QB)
        cols = pl.ds(column, QB)
        low = thrice(lows[:, cols], heads)
        high = thrice(highs[:, cols], heads)
        queries = stacked(q_masked, cols)
        tile0 = first_tile[block]

        def tile_step(step, carry):
            highest, total, accs = carry
            base = pl.multiple_of((tile0 + step) * KT, KT)
            position = key_row + base
            allowed = (position >= low) & (position < high)
            scores = mm_nt(keys_ref[pl.ds(base, KT), :], queries)
            scores = jnp.where(allowed, scores, masked_score)
            newer = jnp.maximum(highest, jnp.max(scores, axis=0, keepdims=True))
            weights = jnp.exp(scores - newer)
            decay = jnp.exp(highest - newer)
            total = total * decay + jnp.sum(weights, axis=0, keepdims=True)
            low_weights = weights.astype(bf16)
            done = []
            for h in range(heads):
                at = slice(h * QB, (h + 1) * QB)
                done.append(
                    accs[h] * decay[:, at]
                    + mm(vt_ref[h * size : (h + 1) * size, pl.ds(base, KT)], low_weights[:, at])
                )
            return newer, total, tuple(done)

        empty = (
            jnp.full((1, wide), masked_score, f32),
            jnp.zeros((1, wide), f32),
            tuple(jnp.zeros((size, QB), f32) for h in range(heads)),
        )
        highest, total, accs = lax.fori_loop(0, tile_count[block], tile_step, empty)
        inverse = 1.0 / total
        logsum = highest + jnp.log(total)
        for h in range(heads):
            at = slice(h * QB, (h + 1) * QB)
            ot_out[h * size : (h + 1) * size, cols] = accs[h] * inverse[:, at]
            lse_out[h : h + 1, cols] = logsum[:, at]
        return unused

    lax.fori_loop(0, length // QB, block_step, 0)
    for rel, piece in enumerate((o0, o1, o2, o3)):
        place = pl.multiple_of((me ^ rel) * rows, rows)
        piece[...] = ot_out[:, pl.ds(place, rows)].astype(bf16)
        o_full[:, rel * rows : (rel + 1) * rows] = piece[...]


def cross_backward_kernel(
    heads,
    index,
    first_tile,
    tile_count,
    lows,
    highs,
    g0,
    g1,
    g2,
    g3,
    w_out,
    q_masked,
    keys_ref,
    values_ref,
    kt_ref,
    ot_ref,
    lse_ref,
    dq_full,
    q0,
    q1,
    q2,
    q3,
    d_out,
    m0,
    m1,
    m2,
    m3,
    do_masked,
    do_t,
    dq_t,
    dk_acc,
    dv_acc,
):
    me = index[0]
    rows, width = g0.shape[0], w_out.shape[0]
    size = width // heads
    wide = heads * QB
    masks = head_masks(rows, width, heads)
    for rel, part in enumerate((g0, g1, g2, g3)):
        place = pl.multiple_of((me ^ rel) * rows, rows)
        values = part[...]
        fill_masked(do_masked, place, mm_nt(values, w_out[...]), masks)
        do_t[:, pl.ds(place, rows)] = mm_nt(w_out[...], values).astype(bf16).astype(f32)
    dk_acc[...] = jnp.zeros_like(dk_acc)
    dv_acc[...] = jnp.zeros_like(dv_acc)
    length = q_masked.shape[1]
    key_row = lax.broadcasted_iota(jnp.int32, (KT, wide), 0)

    def block_step(block, unused):
        column = pl.multiple_of(block * QB, QB)
        cols = pl.ds(column, QB)
        low = thrice(lows[:, cols], heads)
        high = thrice(highs[:, cols], heads)
        stacked_q = stacked(q_masked, cols)
        stacked_o = stacked(do_masked, cols)
        logsum = head_rows(lse_ref, cols)
        inner = do_t[:, cols] * ot_ref[:, cols]
        inner = jnp.concatenate(
            [
                jnp.sum(inner[h * size : (h + 1) * size], axis=0, keepdims=True)
                for h in range(heads)
            ],
            axis=1,
        )
        tile0 = first_tile[block]

        def tile_step(step, carry):
            base = pl.multiple_of((tile0 + step) * KT, KT)
            position = key_row + base
            allowed = (position >= low) & (position < high)
            scores = mm_nt(keys_ref[pl.ds(base, KT), :], stacked_q)
            weights = jnp.exp(jnp.where(allowed, scores - logsum, masked_score))
            upstream = mm_nt(values_ref[pl.ds(base, KT), :], stacked_o)
            grads = (weights * (upstream - inner)).astype(bf16)
            dk_acc[pl.ds(base, KT), :] += mm(grads, stacked_q)
            dv_acc[pl.ds(base, KT), :] += mm(weights.astype(bf16), stacked_o)
            return tuple(
                carry[h]
                + mm(
                    kt_ref[h * size : (h + 1) * size, pl.ds(base, KT)],
                    grads[:, h * QB : (h + 1) * QB],
                )
                for h in range(heads)
            )

        empty = tuple(jnp.zeros((size, QB), f32) for h in range(heads))
        pieces = lax.fori_loop(0, tile_count[block], tile_step, empty)
        for h in range(heads):
            dq_t[h * size : (h + 1) * size, cols] = pieces[h].astype(bf16)
        return unused

    lax.fori_loop(0, length // QB, block_step, 0)
    for rel, piece in enumerate((q0, q1, q2, q3)):
        place = pl.multiple_of((me ^ rel) * rows, rows)
        piece[...] = dq_t[:, pl.ds(place, rows)]
        dq_full[:, rel * rows : (rel + 1) * rows] = piece[...]
    mem_rows = m0.shape[0]
    for rel, piece in enumerate((m0, m1, m2, m3)):
        place = pl.multiple_of((me ^ rel) * mem_rows, mem_rows)
        both = jnp.concatenate(
            [dk_acc[pl.ds(place, mem_rows), :], dv_acc[pl.ds(place, mem_rows), :]], axis=1
        ).astype(bf16)
        piece[...] = both
        d_out[pl.ds(place, mem_rows), :] = both


def out_norm_kernel(o0, o1, o2, o3, w0, w1, w2, w3, resid, gain, h_out, n_out):
    total = resid[...].astype(f32)
    for piece, weight in ((o0, w0), (o1, w1), (o2, w2), (o3, w3)):
        total = total + mm_tn(piece[...], weight[...])
    h_out[...] = total
    n_out[...] = (total * rms_scale(total) * gain[...]).astype(bf16)


def norm_back(values, gain, upstream):
    scale = rms_scale(values)
    weighted = gain * upstream
    gain_grad = jnp.sum(upstream * values * scale, axis=0, keepdims=True)
    inner = jnp.mean(weighted * values, axis=-1, keepdims=True)
    return scale * weighted - values * (scale * scale * scale * inner), gain_grad


def ffn_norm_back_kernel(
    mine, near, far, values, gain, upstream, d_out, g_out, gain_out
):
    incoming = mine[...] + near[...].astype(f32) + far[...].astype(f32)
    grad, gain_grad = norm_back(values[...], gain[...], incoming)
    total = upstream[...].astype(f32) + grad
    d_out[...] = total
    g_out[...] = total.astype(bf16)
    gain_out[...] = gain_grad


def cross_norm_back_kernel(
    index, d0, d1, d2, d3, weights, values, gain, upstream, d_out, g_out, gain_out
):
    me = index[0]
    incoming = jnp.zeros(values.shape, f32)
    for rel, piece in enumerate((d0, d1, d2, d3)):
        incoming = incoming + mm_tn(piece[...], weights[me ^ rel])
    grad, gain_grad = norm_back(values[...], gain[...], incoming)
    total = upstream[...] + grad
    d_out[...] = total
    g_out[...] = total.astype(bf16)
    gain_out[...] = gain_grad


def self_norm_back_kernel(
    index, d0, d1, d2, d3, w_query, w_key, w_value, values, gain, upstream, d_out, gain_out
):
    me = index[0]
    incoming = jnp.zeros(values.shape, f32)
    for n, weight in enumerate((w_query, w_key, w_value)):
        for rel, piece in enumerate((d0, d1, d2, d3)):
            incoming = incoming + mm_tn(piece[n], weight[me ^ rel])
    grad, gain_grad = norm_back(values[...].astype(f32), gain[...], incoming)
    d_out[...] = upstream[...] + grad
    gain_out[...] = gain_grad


def memory_grad_kernel(index, m0, m1, m2, m3, w_key, w_value, out):
    me = index[0]
    total = None
    for rel, piece in enumerate((m0, m1, m2, m3)):
        weight = jnp.concatenate([w_key[me ^ rel], w_value[me ^ rel]], axis=0)
        term = mm(piece[...], weight)
        total = term if total is None else total + term
    out[...] = total


def ffn_kernel(
    c0,
    c1,
    c2,
    c3,
    g0,
    g1,
    g2,
    g3,
    w_gate,
    w_up,
    w_down,
    hidden_out,
    dgate_out,
    dup_out,
    x0,
    x1,
    x2,
    x3,
):
    scale = math.sqrt(2.0 / math.pi)
    rows = c0.shape[0]
    parts = ((c0, g0, x0), (c1, g1, x1), (c2, g2, x2), (c3, g3, x3))
    for rel, (c_ref, g_ref, x_ref) in enumerate(parts):
        at = slice(rel * rows, (rel + 1) * rows)
        gate = mm(c_ref[...], w_gate[...])
        up = mm(c_ref[...], w_up[...])
        back = mm_nt(g_ref[...], w_down[...])
        square = gate * gate
        bent = jnp.tanh(scale * gate * (1.0 + 0.044715 * square))
        half = 0.5 * (1.0 + bent)
        active = gate * half
        slope = half + 0.5 * gate * (1.0 - bent * bent) * (
            scale * (1.0 + 3.0 * 0.044715 * square)
        )
        hidden_out[at, :] = (active * up).astype(bf16)
        dgate = (back * up * slope).astype(bf16)
        dup = (back * active).astype(bf16)
        dgate_out[at, :] = dgate
        dup_out[at, :] = dup
        x_ref[...] = (mm_nt(dgate, w_gate[...]) + mm_nt(dup, w_up[...])).astype(x_ref.dtype)


def swap(values, bit, axis="narrow"):
    return lax.ppermute(
        values, axis, [(i, i ^ bit) for i in range(lax.axis_size(axis))]
    )


def gather_parts(values):
    far = swap(values, 2)
    near = swap(values, 1)
    return (values, near, far, swap(far, 1))


def exchange(pieces):
    return tuple(swap(piece, rel + 1) for rel, piece in enumerate(pieces))


def after(values, *others):
    return lax.optimization_barrier((values,) + others)[0]


def total_over(values, axis):
    bit = 1
    while bit < lax.axis_size(axis):
        values = values + swap(values, bit, axis)
        bit *= 2
    return values


def rows_sum(grads):
    summed = lax.psum(tuple(g.astype(bf16) for g in grads), "rows")
    return tuple(v.astype(f32) for v in summed)


def rows_sum_halves(values):
    place = lax.axis_index("rows")
    bit = 1
    while bit < lax.axis_size("rows"):
        half = values.shape[0] // 2
        mine = (place // bit) % 2
        send = lax.dynamic_slice_in_dim(values, (1 - mine) * half, half, 0).astype(bf16)
        keep = lax.dynamic_slice_in_dim(values, mine * half, half, 0)
        values = keep + swap(send, bit, "rows").astype(f32)
        bit *= 2
    total = values.astype(bf16)
    while bit > 1:
        bit //= 2
        other = swap(total, bit, "rows")
        upper = (place // bit) % 2 == 1
        total = jnp.where(
            upper, jnp.concatenate([other, total]), jnp.concatenate([total, other])
        )
    return total


def weight_grad(inputs, grads):
    return lax.dot_general(inputs, grads, (((0,), (0,)), ((), ())), preferred_element_type=f32)


def plain(left, right):
    return lax.dot_general(left, right, (((1,), (0,)), ((), ())), preferred_element_type=f32)


def body(
    hidden_in,
    memory,
    cotangent,
    seg_ids,
    mem_lengths,
    norm_self,
    norm_cross,
    norm_ffn,
    bias_table,
    self_query,
    self_key,
    self_value,
    self_out,
    cross_query,
    cross_key,
    cross_value,
    cross_out,
    ffn_gate,
    ffn_up,
    ffn_down,
):
    assert lax.axis_size("narrow") == 4 and hidden_in.shape[1] == 1
    rows, width = hidden_in.shape[0], hidden_in.shape[2]
    length = rows * 4
    mem_rows = memory.shape[0]
    mem_length = mem_rows * 4
    heads = bias_table.shape[1]
    local = self_query.shape[1]
    hidden_local = ffn_gate.shape[1]
    blocks = length // QB
    me = lax.axis_index("narrow").astype(jnp.int32)
    index = me.reshape((1,))

    groups = mem_lengths.shape[1]
    group = jnp.arange(groups, dtype=jnp.int32)
    member = seg_ids[0][None, :] == group[:, None]
    counts = jnp.sum(member.astype(jnp.int32), axis=1)
    earlier = group[None, :] < group[:, None]
    tables = jnp.stack([counts, mem_lengths[0]])
    begins = jnp.sum(jnp.where(earlier[None], tables[:, None, :], 0), axis=2)
    bounds = jnp.concatenate([begins, begins[1:] + tables[1:]], axis=0)
    placed = jnp.sum(jnp.where(member[None], bounds[:, :, None], 0), axis=1)
    starts, lows, highs = placed[0:1], placed[1:2], placed[2:3]
    first_tile = jnp.min(lows.reshape(blocks, QB), axis=1) // KT
    tile_count = (jnp.max(highs.reshape(blocks, QB), axis=1) + KT - 1) // KT - first_tile

    hidden_2d = hidden_in.reshape(rows, width)
    memory_2d = memory.reshape(mem_rows, width)
    cotangent_2d = cotangent.reshape(rows, width)
    gain_self = norm_self.reshape(1, width)
    gain_cross = norm_cross.reshape(1, width)
    gain_ffn = norm_ffn.reshape(1, width)

    tokens = hidden_2d.astype(f32)
    normed_a = (tokens * rms_scale(tokens) * gain_self).astype(bf16)
    parts_a = gather_parts(normed_a)
    outs_self = gather_parts(self_out)
    memory_all = lax.all_gather(memory_2d, "narrow", axis=0, tiled=True)
    (bias,) = run(
        functools.partial(bias_kernel, heads), "bias", [bias_table], [],
        [shape((WIDE, heads * QB), f32)], flops=1e6, moved=6e5,
    )
    part_shape = shape((local, rows), bf16)

    (q_a, k_a, v_a, kt_a, ot_a, lse_a, o_a, *send_a) = run(
        functools.partial(self_forward_kernel, heads),
        "self_forward",
        [index],
        [starts, bias, *parts_a, self_query, self_key, self_value, self_key.T, self_value.T],
        [
            shape((heads, length, local), bf16),
            shape((length, local), bf16),
            shape((length, local), bf16),
            shape((local, length), bf16),
            shape((local, length), f32),
            shape((8, length), f32),
            shape((local, length), bf16),
            part_shape,
            part_shape,
            part_shape,
            part_shape,
        ],
        [pltpu.VMEM((local, length), bf16)],
        flops=5e9,
        moved=8e6,
    )
    recv_a = exchange(send_a[1:])
    first_h, normed_b = run(
        out_norm_kernel, "self_out_norm", [],
        [send_a[0], *recv_a, *outs_self, hidden_2d, gain_cross],
        [shape((rows, width), f32), shape((rows, width), bf16)],
        flops=4e8, moved=4e6,
    )
    parts_b = gather_parts(normed_b)

    key_b, value_b, kt_b, vt_b = project_memory(
        memory_all, cross_key, cross_value, cross_key.T, cross_value.T
    )
    later = lax.optimization_barrier(
        (
            cross_query.T, self_query.T, self_key.T, self_value.T,
            cross_key.T, cross_value.T, memory_all[:8],
        )
    )
    whole_w = [lax.all_gather(w, "narrow", axis=0, tiled=False) for w in later[:6]]

    (q_b, ot_b, lse_b, o_b, *send_b) = run(
        functools.partial(cross_forward_kernel, heads),
        "cross_forward",
        [index, first_tile, tile_count],
        [lows, highs, *parts_b, cross_query, key_b, vt_b],
        [
            shape((heads, length, local), bf16),
            shape((local, length), f32),
            shape((8, length), f32),
            shape((local, length), bf16),
            part_shape,
            part_shape,
            part_shape,
            part_shape,
        ],
        flops=8e9,
        moved=1e7,
    )
    outs_cross = gather_parts(after(cross_out, parts_b[3]))
    parts_g = gather_parts(after(cotangent_2d, outs_cross[2]))
    recv_b = exchange(send_b[1:])
    second_h, normed_c = run(
        out_norm_kernel, "cross_out_norm", [],
        [send_b[0], *recv_b, *outs_cross, first_h, gain_ffn],
        [shape((rows, width), f32), shape((rows, width), bf16)],
        flops=4e8, moved=4e6,
    )
    parts_c = gather_parts(normed_c)

    hidden, dgate, dup, x0, x1, x2, x3 = run(
        ffn_kernel,
        "ffn",
        [],
        [*parts_c, *parts_g, ffn_gate, ffn_up, ffn_down],
        [
            shape((length, hidden_local), bf16),
            shape((length, hidden_local), bf16),
            shape((length, hidden_local), bf16),
            shape((rows, width), f32),
            shape((rows, width), bf16),
            shape((rows, width), f32),
            shape((rows, width), bf16),
        ],
        flops=5e9,
        moved=1.2e7,
    )
    near1 = swap(x1, 1)
    near3 = swap(x3, 1)
    far = swap((x2 + near3.astype(f32)).astype(bf16), 2)
    grad_second, grad_second_low, gain_grad_c = run(
        ffn_norm_back_kernel, "ffn_norm_back", [],
        [x0, near1, far, second_h, gain_ffn, cotangent_2d],
        [shape((rows, width), f32), shape((rows, width), bf16), shape((1, width), f32)],
        flops=1e7, moved=4e6,
    )
    parts_gc = gather_parts(grad_second_low)

    whole_c = jnp.concatenate(parts_c, axis=0)
    whole_g = jnp.concatenate(parts_g, axis=0)
    ffn_grads = rows_sum(
        (weight_grad(whole_c, dgate), weight_grad(whole_c, dup), weight_grad(hidden, whole_g))
    )

    (dq_b, *rest_b) = run(
        functools.partial(cross_backward_kernel, heads),
        "cross_backward",
        [index, first_tile, tile_count],
        [lows, highs, *parts_gc, cross_out, q_b, key_b, value_b, kt_b, ot_b, lse_b],
        [shape((local, length), bf16)]
        + [part_shape] * 4
        + [shape((mem_length, 2 * local), bf16)]
        + [shape((mem_rows, 2 * local), bf16)] * 4,
        [
            pltpu.VMEM((heads, length, local), bf16),
            pltpu.VMEM((local, length), f32),
            pltpu.VMEM((local, length), bf16),
            pltpu.VMEM((mem_length, local), f32),
            pltpu.VMEM((mem_length, local), f32),
        ],
        flops=1.6e10,
        moved=2e7,
    )
    send_qb, d_b, send_m = rest_b[:4], rest_b[4], rest_b[5:]
    recv_qb = exchange(send_qb[1:])
    grad_first, grad_first_low, gain_grad_b = run(
        cross_norm_back_kernel, "cross_norm_back", [index],
        [send_qb[0], *recv_qb, whole_w[0], first_h, gain_cross, grad_second],
        [shape((rows, width), f32), shape((rows, width), bf16), shape((1, width), f32)],
        flops=4e8, moved=5e6,
    )
    parts_ga = gather_parts(grad_first_low)

    whole_b = jnp.concatenate(parts_b, axis=0)
    whole_gc = jnp.concatenate(parts_gc, axis=0)
    cross_grads = rows_sum_halves(
        jnp.concatenate(
            [plain(dq_b, whole_b), weight_grad(d_b, memory_all), plain(o_b, whole_gc)], axis=0
        )
    )

    share = lax.dot_general(
        after(hidden, parts_gc[3]), ffn_down, (((1,), (0,)), ((), ())),
        preferred_element_type=f32,
    ).reshape(4, rows, width)
    out1 = swap(share[1].astype(bf16), 1)
    out3 = swap(share[3].astype(bf16), 1)
    out2 = swap((share[2] + out3.astype(f32)).astype(bf16), 2)
    layer_out = (second_h + (share[0] + out1.astype(f32)) + out2.astype(f32)).astype(bf16)

    recv_m = exchange([after(piece, parts_ga[3]) for piece in send_m[1:]])
    (grad_memory,) = run(
        memory_grad_kernel, "memory_grad", [index],
        [send_m[0], *recv_m, whole_w[4], whole_w[5]],
        [shape((mem_rows, width), f32)],
        flops=2.4e9, moved=1e7,
    )

    (d_a, *rest_a) = run(
        functools.partial(self_backward_kernel, heads),
        "self_backward",
        [index],
        [starts, bias, *parts_ga, self_out, q_a, k_a, v_a, kt_a, ot_a, lse_a],
        [shape((3 * local, length), bf16)]
        + [shape((3, local, rows), bf16)] * 4
        + [shape((WIDE, heads * QB), f32)],
        [
            pltpu.VMEM((heads, length, local), bf16),
            pltpu.VMEM((local, length), f32),
            pltpu.VMEM((local, length), bf16),
            pltpu.VMEM((length, local), f32),
            pltpu.VMEM((length, local), f32),
        ],
        flops=8e9,
        moved=1e7,
    )
    send_pa, bias_sum = rest_a[:4], rest_a[4]
    whole_a = jnp.concatenate(parts_a, axis=0)
    whole_ga = jnp.concatenate(parts_ga, axis=0)
    self_grads = rows_sum_halves(
        jnp.concatenate([plain(d_a, whole_a), plain(o_a, whole_ga)], axis=0)
    )

    recv_pa = exchange(send_pa[1:])
    grad_input, gain_grad_a = run(
        self_norm_back_kernel, "self_norm_back", [index],
        [send_pa[0], *recv_pa, *whole_w[1:4], hidden_2d, gain_self, grad_first],
        [shape((rows, width), f32), shape((1, width), f32)],
        flops=1.2e9, moved=8e6,
    )

    (bias_parts,) = run(
        functools.partial(bias_grad_kernel, heads), "bias_grad", [], [bias_sum],
        [shape((heads, len(bucket_starts), QB), f32)], flops=1e7, moved=6e5,
    )
    grad_table = jnp.sum(bias_parts, axis=2).T

    gains = total_over(jnp.concatenate([gain_grad_a, gain_grad_b, gain_grad_c], axis=0), "narrow")
    small = total_over(
        jnp.concatenate([gains.reshape(-1), grad_table.reshape(-1)]), "rows"
    )
    gain_totals = small[: 3 * width].reshape(3, width)
    table_total = small[3 * width :].reshape(grad_table.shape)

    def finished(total):
        columns = [total[n * local : (n + 1) * local].astype(f32).T for n in range(3)]
        return columns + [total[3 * local :].astype(f32)]

    cross_done = finished(cross_grads)
    self_done = finished(self_grads)

    return (
        layer_out.reshape(rows, 1, width),
        grad_input.reshape(rows, 1, width),
        grad_memory.reshape(mem_rows, 1, width),
        gain_totals[0],
        gain_totals[1],
        gain_totals[2],
        table_total,
        *self_done,
        *cross_done,
        ffn_grads[0],
        ffn_grads[1],
        ffn_grads[2],
    )


def solution(mesh):
    in_specs = (
        P("narrow", "rows", None),
        P("narrow", "rows", None),
        P("narrow", "rows", None),
        P("rows", None),
        P("rows", None),
        P(),
        P(),
        P(),
        P(None, "narrow"),
        P(None, "narrow"),
        P(None, "narrow"),
        P(None, "narrow"),
        P("narrow", None),
        P(None, "narrow"),
        P(None, "narrow"),
        P(None, "narrow"),
        P("narrow", None),
        P(None, "narrow"),
        P(None, "narrow"),
        P("narrow", None),
    )
    out_specs = (
        P("narrow", "rows", None),
        P("narrow", "rows", None),
        P("narrow", "rows", None),
        P(),
        P(),
        P(),
        P(None, "narrow"),
        P(None, "narrow"),
        P(None, "narrow"),
        P(None, "narrow"),
        P("narrow", None),
        P(None, "narrow"),
        P(None, "narrow"),
        P(None, "narrow"),
        P("narrow", None),
        P(None, "narrow"),
        P(None, "narrow"),
        P("narrow", None),
    )
    return jax.shard_map(body, mesh=mesh, in_specs=in_specs, out_specs=out_specs, check_vma=False)
```

```python
import functools
import math

import jax
import jax.numpy as jnp
import numpy as np
from jax import lax
from jax.experimental import pallas as pl
from jax.experimental.pallas import tpu as pltpu
from jax.sharding import PartitionSpec as P


f32 = jnp.float32
bf16 = jnp.bfloat16
masked_score = -1e30
epsilon = 1e-06
bucket_edges = [int(v) for v in np.ceil(16.0 * 8.0 ** (np.arange(1, 16) / 16.0))]
bucket_starts = list(range(17)) + bucket_edges

QB = 128
KT = 256
MB = 512
BAND = 256
WIDE = BAND + QB


def mm(left, right):
    return lax.dot_general(left, right, (((1,), (0,)), ((), ())), preferred_element_type=f32)


def mm_nt(left, right):
    return lax.dot_general(left, right, (((1,), (1,)), ((), ())), preferred_element_type=f32)


def mm_tn(left, right):
    return lax.dot_general(left, right, (((0,), (0,)), ((), ())), preferred_element_type=f32)


def vmem(count):
    return [pl.BlockSpec(memory_space=pltpu.VMEM)] * count


def smem(count):
    return [pl.BlockSpec(memory_space=pltpu.SMEM)] * count


def shape(dims, kind):
    return jax.ShapeDtypeStruct(dims, kind)


def run(kernel, scalars, arrays, outs, scratch=(), flops=0, moved=0, blocks=None):
    if blocks is None:
        grid, in_specs, out_specs = (), vmem(len(arrays)), vmem(len(outs))
    else:
        grid = (1,)
        in_specs, out_specs = (
            [pl.BlockSpec(v.shape, lambda i, n=len(v.shape): (0,) * n) for v in group]
            for group in (arrays, outs)
        )
        for place, (block, position) in blocks.items():
            in_specs[place] = pl.BlockSpec(block, lambda i, at=position: at)
    return pl.pallas_call(
        kernel,
        grid=grid,
        in_specs=smem(len(scalars)) + in_specs,
        out_specs=out_specs,
        out_shape=list(outs),
        scratch_shapes=list(scratch),
        compiler_params=pltpu.CompilerParams(vmem_limit_bytes=60 * 1024 * 1024),
        cost_estimate=pl.CostEstimate(
            flops=int(flops), bytes_accessed=int(moved), transcendentals=0
        ),
    )(*scalars, *arrays)


def head_masks(rows, width, heads):
    lane = lax.broadcasted_iota(jnp.int32, (rows, width), 1)
    size = width // heads
    return [(lane >= h * size) & (lane < (h + 1) * size) for h in range(heads)]


def rms_scale(values):
    return lax.rsqrt(jnp.mean(values * values, axis=-1, keepdims=True) + epsilon)


def band_distance():
    row = lax.broadcasted_iota(jnp.int32, (WIDE, QB), 0)
    lane = lax.broadcasted_iota(jnp.int32, (WIDE, QB), 1)
    return lane + BAND - row


def bias_kernel(heads, table, out):
    distance = band_distance()
    values = [jnp.full((WIDE, QB), table[0, h], f32) for h in range(heads)]
    for bucket in range(1, len(bucket_starts)):
        reached = distance >= bucket_starts[bucket]
        values = [jnp.where(reached, table[bucket, h], values[h]) for h in range(heads)]
    for h in range(heads):
        out[:, h * QB : (h + 1) * QB] = jnp.where(distance >= 0, values[h], masked_score)


def bias_grad_kernel(heads, grads, out):
    distance = band_distance()
    count = len(bucket_starts)

    def head_step(h):
        values = grads[:, pl.ds(pl.multiple_of(h * QB, QB), QB)]
        for bucket in range(count):
            inside = distance >= bucket_starts[bucket]
            if bucket + 1 < count:
                inside = inside & (distance < bucket_starts[bucket + 1])
            out[h, bucket : bucket + 1, :] = jnp.sum(
                jnp.where(inside, values, 0.0), axis=0, keepdims=True
            )

    each(heads, head_step)


def fill_masked(target, place, values, masks):
    for h, mask in enumerate(masks):
        target[h, pl.ds(place, values.shape[0]), :] = jnp.where(mask, values, 0.0).astype(bf16)


def stacked(masked, cols):
    return jnp.concatenate([masked[h, cols, :] for h in range(masked.shape[0])], axis=0)


def thrice(row, count):
    return jnp.concatenate([row] * count, axis=1)


def head_rows(ref, cols, heads):
    return jnp.concatenate([ref[h : h + 1, cols] for h in range(heads)], axis=1)


def place_parts(parts, whole):
    rows = parts[0].shape[0]
    for rel, part in enumerate(parts):
        whole[rel * rows : (rel + 1) * rows, :] = part[...]


def send_parts(source, full, pieces, me):
    rows = pieces[0].shape[1]
    for rel, piece in enumerate(pieces):
        place = pl.multiple_of((me ^ rel) * rows, rows)
        piece[...] = source[:, pl.ds(place, rows)].astype(bf16)
        full[:, rel * rows : (rel + 1) * rows] = piece[...]


def each(count, step, unroll=1):
    def wrapped(n, unused):
        step(n)
        return unused

    lax.fori_loop(0, count, wrapped, 0, unroll=unroll)


def self_forward_kernel(
    heads,
    index,
    starts,
    bias,
    a0,
    a1,
    a2,
    a3,
    w_query,
    w_key,
    w_value,
    w_key_t,
    w_value_t,
    whole,
    q_masked,
    k_out,
    v_out,
    kt_out,
    ot_out,
    lse_out,
    o_full,
    o0,
    o1,
    o2,
    o3,
    vt,
):
    me = index[0]
    rows, width = a0.shape[0], w_query.shape[1]
    size = width // heads
    masks = head_masks(rows, width, heads)
    place_parts((a0, a1, a2, a3), whole)
    k_out[0:BAND, :] = jnp.zeros((BAND, width), bf16)
    v_out[0:BAND, :] = jnp.zeros((BAND, width), bf16)
    kt_out[:, 0:BAND] = jnp.zeros((width, BAND), bf16)
    vt[:, 0:BAND] = jnp.zeros((width, BAND), bf16)

    def part_step(rel):
        values = whole[pl.ds(pl.multiple_of(rel * rows, rows), rows), :]
        place = pl.multiple_of((me ^ rel) * rows, rows)
        behind = pl.ds(pl.multiple_of(place + BAND, QB), rows)
        fill_masked(q_masked, place, mm(values, w_query[...]), masks)
        k_out[behind, :] = mm(values, w_key[...]).astype(bf16)
        v_out[behind, :] = mm(values, w_value[...]).astype(bf16)
        kt_out[:, behind] = mm_nt(w_key_t[...], values).astype(bf16)
        vt[:, behind] = mm_nt(w_value_t[...], values).astype(bf16)

    each(4, part_step)
    band_row = lax.broadcasted_iota(jnp.int32, (WIDE, heads * QB), 0)

    def block_step(block):
        low = pl.multiple_of(block * QB, QB)
        cols, window = pl.ds(low, QB), pl.ds(low, WIDE)
        allowed = band_row >= thrice(starts[:, cols], heads) - (low - BAND)
        scores = mm_nt(k_out[window, :], stacked(q_masked, cols)) + bias[...]
        scores = jnp.where(allowed, scores, masked_score)
        highest = jnp.max(scores, axis=0, keepdims=True)
        exponent = jnp.exp(scores - highest)
        total = jnp.sum(exponent, axis=0, keepdims=True)
        weights = (exponent * (1.0 / total)).astype(bf16)
        logsum = highest + jnp.log(total)
        for h in range(heads):
            part = slice(h * size, (h + 1) * size)
            at = slice(h * QB, (h + 1) * QB)
            ot_out[part, cols] = mm(vt[part, window], weights[:, at])
            lse_out[h : h + 1, cols] = logsum[:, at]

    each(q_masked.shape[1] // QB, block_step)
    send_parts(ot_out, o_full, (o0, o1, o2, o3), me)


def inner_products(do_t, ot_ref, cols, heads):
    both = do_t[:, cols] * ot_ref[:, cols]
    size = both.shape[0] // heads
    return jnp.concatenate(
        [jnp.sum(both[h * size : (h + 1) * size], axis=0, keepdims=True) for h in range(heads)],
        axis=1,
    )


def output_grads(whole, w_out, do_masked, do_t, me, heads):
    length, width = do_masked.shape[1], w_out.shape[0]
    rows = length // 4
    masks = head_masks(rows, width, heads)

    def part_step(rel):
        values = whole[pl.ds(pl.multiple_of(rel * rows, rows), rows), :]
        place = pl.multiple_of((me ^ rel) * rows, rows)
        fill_masked(do_masked, place, mm_nt(values, w_out[...]), masks)
        do_t[:, pl.ds(place, rows)] = mm_nt(w_out[...], values).astype(bf16).astype(f32)

    each(4, part_step)


def self_backward_kernel(
    heads,
    index,
    starts,
    bias,
    g0,
    g1,
    g2,
    g3,
    w_out,
    q_masked,
    keys_ref,
    values_ref,
    kt_ref,
    ot_ref,
    lse_ref,
    whole,
    d_full,
    p0,
    p1,
    p2,
    p3,
    bias_out,
    do_masked,
    do_t,
    dq_t,
    dk_acc,
    dv_acc,
):
    me = index[0]
    rows, width = g0.shape[0], w_out.shape[0]
    size = width // heads
    place_parts((g0, g1, g2, g3), whole)
    output_grads(whole, w_out, do_masked, do_t, me, heads)
    bias_out[...] = jnp.zeros_like(bias_out)
    dk_acc[...] = jnp.zeros_like(dk_acc)
    dv_acc[...] = jnp.zeros_like(dv_acc)
    band_row = lax.broadcasted_iota(jnp.int32, (WIDE, heads * QB), 0)

    def block_step(block):
        low = pl.multiple_of(block * QB, QB)
        cols, window = pl.ds(low, QB), pl.ds(low, WIDE)
        allowed = band_row >= thrice(starts[:, cols], heads) - (low - BAND)
        stacked_q = stacked(q_masked, cols)
        stacked_o = stacked(do_masked, cols)
        scores = mm_nt(keys_ref[window, :], stacked_q) + bias[...]
        scores = scores - head_rows(lse_ref, cols, heads)
        weights = jnp.exp(jnp.where(allowed, scores, masked_score))
        inner = inner_products(do_t, ot_ref, cols, heads)
        grads = (weights * (mm_nt(values_ref[window, :], stacked_o) - inner)).astype(bf16)
        bias_out[...] += grads.astype(f32)
        for h in range(heads):
            part = slice(h * size, (h + 1) * size)
            dq_t[part, cols] = mm(kt_ref[part, window], grads[:, h * QB : (h + 1) * QB]).astype(
                bf16
            )
        dk_acc[window, :] += mm(grads, stacked_q)
        dv_acc[window, :] += mm(weights.astype(bf16), stacked_o)

    each(q_masked.shape[1] // QB, block_step)
    for rel, piece in enumerate((p0, p1, p2, p3)):
        place = pl.multiple_of((me ^ rel) * rows, rows)
        behind = pl.ds(pl.multiple_of(place + BAND, QB), rows)
        piece[0] = dq_t[:, pl.ds(place, rows)]
        piece[1] = dk_acc[behind, :].T.astype(bf16)
        piece[2] = dv_acc[behind, :].T.astype(bf16)
        for n in range(3):
            d_full[n * width : (n + 1) * width, rel * rows : (rel + 1) * rows] = piece[n]


def memory_kernel(x, w_key, w_value, w_key_t, w_value_t, k_out, v_out, kt_out, vt_out):
    values = x[...]
    k_out[...] = mm(values, w_key[...]).astype(bf16)
    v_out[...] = mm(values, w_value[...]).astype(bf16)
    kt_out[...] = mm_nt(w_key_t[...], values).astype(bf16)
    vt_out[...] = mm_nt(w_value_t[...], values).astype(bf16)


def project_memory(memory_all, w_key, w_value, w_key_t, w_value_t):
    count, width = memory_all.shape
    local = w_key.shape[1]
    return pl.pallas_call(
        memory_kernel,
        name="project_memory",
        grid=(count // MB,),
        in_specs=[
            pl.BlockSpec((MB, width), lambda i: (i, 0)),
            pl.BlockSpec((width, local), lambda i: (0, 0)),
            pl.BlockSpec((width, local), lambda i: (0, 0)),
            pl.BlockSpec((local, width), lambda i: (0, 0)),
            pl.BlockSpec((local, width), lambda i: (0, 0)),
        ],
        out_specs=[
            pl.BlockSpec((MB, local), lambda i: (i, 0)),
            pl.BlockSpec((MB, local), lambda i: (i, 0)),
            pl.BlockSpec((local, MB), lambda i: (0, i)),
            pl.BlockSpec((local, MB), lambda i: (0, i)),
        ],
        out_shape=[
            shape((count, local), bf16),
            shape((count, local), bf16),
            shape((local, count), bf16),
            shape((local, count), bf16),
        ],
        cost_estimate=pl.CostEstimate(
            flops=8 * count * width * local, bytes_accessed=2 * count * (width + 4 * local),
            transcendentals=0,
        ),
    )(memory_all, w_key, w_value, w_key_t, w_value_t)


def cross_forward_kernel(
    heads,
    index,
    first_tile,
    tile_count,
    lows,
    highs,
    b0,
    b1,
    b2,
    b3,
    w_query,
    keys_ref,
    vt_ref,
    whole,
    q_masked,
    ot_out,
    lse_out,
    o_full,
    o0,
    o1,
    o2,
    o3,
):
    me = index[0]
    rows, width = b0.shape[0], w_query.shape[1]
    size = width // heads
    wide = heads * QB
    masks = head_masks(rows, width, heads)
    place_parts((b0, b1, b2, b3), whole)

    def part_step(rel):
        values = whole[pl.ds(pl.multiple_of(rel * rows, rows), rows), :]
        place = pl.multiple_of((me ^ rel) * rows, rows)
        fill_masked(q_masked, place, mm(values, w_query[...]), masks)

    each(4, part_step)
    length = q_masked.shape[1]
    key_row = lax.broadcasted_iota(jnp.int32, (KT, wide), 0)

    def block_step(block, unused):
        column = pl.multiple_of(block * QB, QB)
        cols = pl.ds(column, QB)
        low = thrice(lows[:, cols], heads)
        high = thrice(highs[:, cols], heads)
        queries = stacked(q_masked, cols)
        tile0 = first_tile[block]

        def tile_step(step, carry):
            highest, total, accs = carry
            base = pl.multiple_of((tile0 + step) * KT, KT)
            position = key_row + base
            allowed = (position >= low) & (position < high)
            scores = mm_nt(keys_ref[pl.ds(base, KT), :], queries)
            scores = jnp.where(allowed, scores, masked_score)
            newer = jnp.maximum(highest, jnp.max(scores, axis=0, keepdims=True))
            weights = jnp.exp(scores - newer)
            decay = jnp.exp(highest - newer)
            total = total * decay + jnp.sum(weights, axis=0, keepdims=True)
            low_weights = weights.astype(bf16)
            done = []
            for h in range(heads):
                at = slice(h * QB, (h + 1) * QB)
                done.append(
                    accs[h] * decay[:, at]
                    + mm(vt_ref[h * size : (h + 1) * size, pl.ds(base, KT)], low_weights[:, at])
                )
            return newer, total, tuple(done)

        empty = (
            jnp.full((1, wide), masked_score, f32),
            jnp.zeros((1, wide), f32),
            tuple(jnp.zeros((size, QB), f32) for _ in range(heads)),
        )
        highest, total, accs = lax.fori_loop(0, tile_count[block], tile_step, empty)
        inverse = 1.0 / total
        logsum = highest + jnp.log(total)
        for h in range(heads):
            at = slice(h * QB, (h + 1) * QB)
            ot_out[h * size : (h + 1) * size, cols] = accs[h] * inverse[:, at]
            lse_out[h : h + 1, cols] = logsum[:, at]
        return unused

    lax.fori_loop(0, length // QB, block_step, 0)
    send_parts(ot_out, o_full, (o0, o1, o2, o3), me)


def cross_backward_kernel(
    heads,
    index,
    first_tile,
    tile_count,
    lows,
    highs,
    g0,
    g1,
    g2,
    g3,
    w_out,
    q_masked,
    keys_ref,
    values_ref,
    kt_ref,
    ot_ref,
    lse_ref,
    whole,
    dq_full,
    q0,
    q1,
    q2,
    q3,
    d_out,
    m0,
    m1,
    m2,
    m3,
    do_masked,
    do_t,
    dq_t,
    dk_acc,
    dv_acc,
):
    me = index[0]
    width = w_out.shape[0]
    size = width // heads
    wide = heads * QB
    place_parts((g0, g1, g2, g3), whole)
    output_grads(whole, w_out, do_masked, do_t, me, heads)
    dk_acc[...] = jnp.zeros_like(dk_acc)
    dv_acc[...] = jnp.zeros_like(dv_acc)
    length = q_masked.shape[1]
    key_row = lax.broadcasted_iota(jnp.int32, (KT, wide), 0)

    def block_step(block, unused):
        column = pl.multiple_of(block * QB, QB)
        cols = pl.ds(column, QB)
        low = thrice(lows[:, cols], heads)
        high = thrice(highs[:, cols], heads)
        stacked_q = stacked(q_masked, cols)
        stacked_o = stacked(do_masked, cols)
        logsum = head_rows(lse_ref, cols, heads)
        inner = inner_products(do_t, ot_ref, cols, heads)
        tile0 = first_tile[block]

        def tile_step(step, carry):
            base = pl.multiple_of((tile0 + step) * KT, KT)
            position = key_row + base
            allowed = (position >= low) & (position < high)
            scores = mm_nt(keys_ref[pl.ds(base, KT), :], stacked_q)
            weights = jnp.exp(jnp.where(allowed, scores - logsum, masked_score))
            upstream = mm_nt(values_ref[pl.ds(base, KT), :], stacked_o)
            grads = (weights * (upstream - inner)).astype(bf16)
            dk_acc[pl.ds(base, KT), :] += mm(grads, stacked_q)
            dv_acc[pl.ds(base, KT), :] += mm(weights.astype(bf16), stacked_o)
            return tuple(
                carry[h]
                + mm(
                    kt_ref[h * size : (h + 1) * size, pl.ds(base, KT)],
                    grads[:, h * QB : (h + 1) * QB],
                )
                for h in range(heads)
            )

        empty = tuple(jnp.zeros((size, QB), f32) for _ in range(heads))
        pieces = lax.fori_loop(0, tile_count[block], tile_step, empty)
        for h in range(heads):
            dq_t[h * size : (h + 1) * size, cols] = pieces[h].astype(bf16)
        return unused

    lax.fori_loop(0, length // QB, block_step, 0)
    send_parts(dq_t, dq_full, (q0, q1, q2, q3), me)
    mem_rows = m0.shape[0]

    def out_step(n):
        at = pl.ds(pl.multiple_of(n * KT, KT), KT)
        d_out[at, :] = jnp.concatenate([dk_acc[at, :], dv_acc[at, :]], axis=1).astype(bf16)

    each(d_out.shape[0] // KT, out_step)

    def piece_step(n):
        at = pl.multiple_of(n * KT, KT)
        for rel, piece in enumerate((m0, m1, m2, m3)):
            place = pl.multiple_of((me ^ rel) * mem_rows + at, KT)
            piece[pl.ds(at, KT), :] = d_out[pl.ds(place, KT), :]

    each(mem_rows // KT, piece_step)


def out_norm_kernel(o0, o1, o2, o3, w0, w1, w2, w3, resid, gain, h_out, n_out):
    total = resid[...].astype(f32)
    for piece, weight in ((o0, w0), (o1, w1), (o2, w2), (o3, w3)):
        total = total + mm_tn(piece[...], weight[...])
    h_out[...] = total
    n_out[...] = (total * rms_scale(total) * gain[...]).astype(bf16)


def norm_back(values, gain, upstream):
    scale = rms_scale(values)
    weighted = gain * upstream
    gain_grad = jnp.sum(upstream * values * scale, axis=0, keepdims=True)
    inner = jnp.mean(weighted * values, axis=-1, keepdims=True)
    return scale * weighted - values * (scale * scale * scale * inner), gain_grad


def ffn_norm_back_kernel(
    mine, near, far, values, gain, upstream, d_out, g_out, gain_out
):
    incoming = mine[...] + near[...].astype(f32) + far[...].astype(f32)
    grad, gain_grad = norm_back(values[...], gain[...], incoming)
    total = upstream[...].astype(f32) + grad
    d_out[...] = total
    g_out[...] = total.astype(bf16)
    gain_out[...] = gain_grad


def cross_norm_back_kernel(
    index, d0, d1, d2, d3, weights, values, gain, upstream, d_out, g_out, gain_out
):
    me = index[0]
    incoming = jnp.zeros(values.shape, f32)
    for rel, piece in enumerate((d0, d1, d2, d3)):
        incoming = incoming + mm_tn(piece[...], weights[me ^ rel])
    grad, gain_grad = norm_back(values[...], gain[...], incoming)
    total = upstream[...] + grad
    d_out[...] = total
    g_out[...] = total.astype(bf16)
    gain_out[...] = gain_grad


def self_norm_back_kernel(
    index, d0, d1, d2, d3, weights, values, gain, upstream, d_out, gain_out
):
    me = index[0]
    incoming = jnp.zeros(values.shape, f32)
    for rel, piece in enumerate((d0, d1, d2, d3)):
        both = piece[...].reshape(-1, piece.shape[2])
        incoming = incoming + mm_tn(both, weights[me ^ rel])
    grad, gain_grad = norm_back(values[...].astype(f32), gain[...], incoming)
    d_out[:, 0, :] = upstream[...] + grad
    gain_out[...] = gain_grad


def memory_grad_kernel(index, m0, m1, m2, m3, weights, out):
    me = index[0]
    total = None
    for rel, piece in enumerate((m0, m1, m2, m3)):
        term = mm(piece[...], weights[me ^ rel])
        total = term if total is None else total + term
    out[:, 0, :] = total


def memory_grads(index, parts, weights):
    mem_rows, both = parts[0].shape
    width = weights.shape[2]
    step = mem_rows // 4
    return pl.pallas_call(
        memory_grad_kernel,
        name="memory_grad",
        grid=(4,),
        in_specs=smem(1)
        + [pl.BlockSpec((step, both), lambda i: (i, 0))] * 4
        + [pl.BlockSpec((4, both, width), lambda i: (0, 0, 0))],
        out_specs=pl.BlockSpec((step, 1, width), lambda i: (i, 0, 0)),
        out_shape=shape((mem_rows, 1, width), f32),
        cost_estimate=pl.CostEstimate(
            flops=8 * mem_rows * both * width, bytes_accessed=10 * mem_rows * width,
            transcendentals=0,
        ),
    )(index, *parts, weights)


def ffn_kernel(
    index,
    c0,
    c1,
    c2,
    c3,
    grads,
    w_gate,
    w_up,
    w_down,
    whole_c,
    whole_g,
    hidden_out,
    dgate_out,
    dup_out,
    x0,
    x1,
    x2,
    x3,
    share,
):
    scale = math.sqrt(2.0 / math.pi)
    rows = c0.shape[0]
    place_parts((c0, c1, c2, c3), whole_c)
    me = index[0]

    def part_step(rel):
        at = pl.ds(pl.multiple_of(rel * rows, rows), rows)
        whole_g[at, :] = grads[pl.ds(pl.multiple_of((me ^ rel) * rows, rows), rows), :]
        values = whole_c[at, :]
        gate = mm(values, w_gate[...])
        up = mm(values, w_up[...])
        back = mm_nt(whole_g[at, :], w_down[...])
        square = gate * gate
        bent = jnp.tanh(scale * gate * (1.0 + 0.044715 * square))
        half = 0.5 * (1.0 + bent)
        active = gate * half
        slope = half + 0.5 * gate * (1.0 - bent * bent) * (
            scale * (1.0 + 3.0 * 0.044715 * square)
        )
        hidden_out[at, :] = (active * up).astype(bf16)
        dgate = (back * up * slope).astype(bf16)
        dup = (back * active).astype(bf16)
        dgate_out[at, :] = dgate
        dup_out[at, :] = dup
        share[at, :] = mm_nt(dgate, w_gate[...]) + mm_nt(dup, w_up[...])

    each(4, part_step)
    for rel, piece in enumerate((x0, x1, x2, x3)):
        piece[...] = share[rel * rows : (rel + 1) * rows, :].astype(piece.dtype)


def swap(values, bit, axis="narrow"):
    return lax.ppermute(
        values, axis, [(i, i ^ bit) for i in range(lax.axis_size(axis))]
    )


def gather_parts(values):
    far = swap(values, 2)
    near = swap(values, 1)
    on = swap(far, 1)
    return (values, near, far, on)


def exchange(pieces):
    return tuple(swap(piece, rel + 1) for rel, piece in enumerate(pieces))


def after(values, *others):
    return lax.optimization_barrier((values,) + others)[0]


def total_over(values, axis):
    bit = 1
    while bit < lax.axis_size(axis):
        values = values + swap(values, bit, axis)
        bit *= 2
    return values


def rows_sum(grads):
    summed = lax.psum(tuple(g.astype(bf16) for g in grads), "rows")
    return tuple(v.astype(f32) for v in summed)


def rows_sum_halves(values):
    place = lax.axis_index("rows")
    bit = 1
    while bit < lax.axis_size("rows"):
        half = values.shape[0] // 2
        mine = (place // bit) % 2
        send = lax.dynamic_slice_in_dim(values, (1 - mine) * half, half, 0).astype(bf16)
        keep = lax.dynamic_slice_in_dim(values, mine * half, half, 0)
        values = keep + swap(send, bit, "rows").astype(f32)
        bit *= 2
    total = values.astype(bf16)
    while bit > 1:
        bit //= 2
        other = swap(total, bit, "rows")
        upper = (place // bit) % 2 == 1
        total = jnp.where(
            upper, jnp.concatenate([other, total]), jnp.concatenate([total, other])
        )
    return total


def weight_grad(inputs, grads):
    return lax.dot_general(inputs, grads, (((0,), (0,)), ((), ())), preferred_element_type=f32)


def plain(left, right):
    return lax.dot_general(left, right, (((1,), (0,)), ((), ())), preferred_element_type=f32)


def body(
    hidden_in,
    memory,
    cotangent,
    seg_ids,
    mem_lengths,
    norm_self,
    norm_cross,
    norm_ffn,
    bias_table,
    self_query,
    self_key,
    self_value,
    self_out,
    cross_query,
    cross_key,
    cross_value,
    cross_out,
    ffn_gate,
    ffn_up,
    ffn_down,
):
    assert lax.axis_size("narrow") == 4 and hidden_in.shape[1] == 1
    rows, width = hidden_in.shape[0], hidden_in.shape[2]
    length = rows * 4
    mem_rows = memory.shape[0]
    mem_length = mem_rows * 4
    heads = bias_table.shape[1]
    local = self_query.shape[1]
    hidden_local = ffn_gate.shape[1]
    blocks = length // QB
    me = lax.axis_index("narrow").astype(jnp.int32)
    index = me.reshape((1,))

    groups = mem_lengths.shape[1]
    group = jnp.arange(groups, dtype=jnp.int32)
    member = seg_ids[0][None, :] == group[:, None]
    counts = jnp.sum(member.astype(jnp.int32), axis=1)
    earlier = group[None, :] < group[:, None]
    tables = jnp.stack([counts, mem_lengths[0]])
    begins = jnp.sum(jnp.where(earlier[None], tables[:, None, :], 0), axis=2)
    bounds = jnp.concatenate([begins, begins[1:] + tables[1:]], axis=0)
    placed = jnp.sum(jnp.where(member[None], bounds[:, :, None], 0), axis=1)
    starts, lows, highs = placed[0:1], placed[1:2], placed[2:3]
    first_tile = jnp.min(lows.reshape(blocks, QB), axis=1) // KT
    tile_count = (jnp.max(highs.reshape(blocks, QB), axis=1) + KT - 1) // KT - first_tile

    hidden_2d = hidden_in.reshape(rows, width)
    memory_2d = memory.reshape(mem_rows, width)
    cotangent_2d = cotangent.reshape(rows, width)
    gain_self = norm_self.reshape(1, width)
    gain_cross = norm_cross.reshape(1, width)
    gain_ffn = norm_ffn.reshape(1, width)

    tokens = hidden_2d.astype(f32)
    normed_a = (tokens * rms_scale(tokens) * gain_self).astype(bf16)
    parts_a = gather_parts(normed_a)
    outs_self = gather_parts(self_out)
    memory_all = lax.all_gather(memory_2d, "narrow", axis=0, tiled=True)
    (bias,) = run(
        functools.partial(bias_kernel, heads), [bias_table], [],
        [shape((WIDE, heads * QB), f32)], flops=1e6, moved=6e5,
    )
    part_shape = shape((local, rows), bf16)

    (whole_a, q_a, k_a, v_a, kt_a, ot_a, lse_a, o_a, *send_a) = run(
        functools.partial(self_forward_kernel, heads),
        [index],
        [starts, bias, *parts_a, self_query, self_key, self_value, self_key.T, self_value.T],
        [
            shape((length, width), bf16),
            shape((heads, length, local), bf16),
            shape((BAND + length, local), bf16),
            shape((BAND + length, local), bf16),
            shape((local, BAND + length), bf16),
            shape((local, length), f32),
            shape((8, length), f32),
            shape((local, length), bf16),
            part_shape,
            part_shape,
            part_shape,
            part_shape,
        ],
        [pltpu.VMEM((local, BAND + length), bf16)],
        flops=5e9,
        moved=8e6,
    )
    recv_a = exchange(send_a[1:])
    first_h, normed_b = run(
        out_norm_kernel, [],
        [send_a[0], *recv_a, *outs_self, hidden_2d, gain_cross],
        [shape((rows, width), f32), shape((rows, width), bf16)],
        flops=4e8, moved=4e6,
    )
    parts_b = gather_parts(normed_b)

    key_b, value_b, kt_b, vt_b = project_memory(
        memory_all, cross_key, cross_value, cross_key.T, cross_value.T
    )
    attention_w = jnp.concatenate(
        [self_query.T, self_key.T, self_value.T, cross_query.T], axis=0
    )
    memory_w = jnp.concatenate([cross_key.T, cross_value.T], axis=0)
    cotangent_all = lax.all_gather(
        after(cotangent_2d, memory_all[:8]), "narrow", axis=0, tiled=True
    )
    attention_w = lax.all_gather(
        after(attention_w, cotangent_all[:8]), "narrow", axis=0, tiled=False
    )
    memory_w = lax.all_gather(
        after(memory_w, attention_w[0, :8]), "narrow", axis=0, tiled=False
    )

    (whole_b, q_b, ot_b, lse_b, o_b, *send_b) = run(
        functools.partial(cross_forward_kernel, heads),
        [index, first_tile, tile_count],
        [lows, highs, *parts_b, cross_query, key_b, vt_b],
        [
            shape((length, width), bf16),
            shape((heads, length, local), bf16),
            shape((local, length), f32),
            shape((8, length), f32),
            shape((local, length), bf16),
            part_shape,
            part_shape,
            part_shape,
            part_shape,
        ],
        flops=8e9,
        moved=1e7,
    )
    behind = after(cross_out, parts_b[3])
    outs_cross = (cross_out, *exchange((behind, behind, behind)))
    recv_b = exchange(send_b[1:])
    second_h, normed_c = run(
        out_norm_kernel, [],
        [send_b[0], *recv_b, *outs_cross, first_h, gain_ffn],
        [shape((rows, width), f32), shape((rows, width), bf16)],
        flops=4e8, moved=4e6,
    )
    parts_c = gather_parts(normed_c)

    whole_c, whole_g, hidden, dgate, dup, x0, x1, x2, x3 = run(
        ffn_kernel,
        [index],
        [*parts_c, cotangent_all, ffn_gate, ffn_up, ffn_down],
        [
            shape((length, width), bf16),
            shape((length, width), bf16),
            shape((length, hidden_local), bf16),
            shape((length, hidden_local), bf16),
            shape((length, hidden_local), bf16),
            shape((rows, width), f32),
            shape((rows, width), bf16),
            shape((rows, width), f32),
            shape((rows, width), bf16),
        ],
        [pltpu.VMEM((length, width), f32)],
        flops=5e9,
        moved=1.2e7,
    )
    near1 = swap(x1, 1)
    near3 = swap(x3, 1)
    far = swap((x2 + near3.astype(f32)).astype(bf16), 2)
    grad_second, grad_second_low, gain_grad_c = run(
        ffn_norm_back_kernel, [],
        [x0, near1, far, second_h, gain_ffn, cotangent_2d],
        [shape((rows, width), f32), shape((rows, width), bf16), shape((1, width), f32)],
        flops=1e7, moved=4e6,
    )
    parts_gc = gather_parts(grad_second_low)

    ffn_grads = rows_sum(
        (weight_grad(whole_c, dgate), weight_grad(whole_c, dup), weight_grad(hidden, whole_g))
    )

    (whole_gc, dq_b, *rest_b) = run(
        functools.partial(cross_backward_kernel, heads),
        [index, first_tile, tile_count],
        [lows, highs, *parts_gc, cross_out, q_b, key_b, value_b, kt_b, ot_b, lse_b],
        [shape((length, width), bf16), shape((local, length), bf16)]
        + [part_shape] * 4
        + [shape((mem_length, 2 * local), bf16)]
        + [shape((mem_rows, 2 * local), bf16)] * 4,
        [
            pltpu.VMEM((heads, length, local), bf16),
            pltpu.VMEM((local, length), f32),
            pltpu.VMEM((local, length), bf16),
            pltpu.VMEM((mem_length, local), f32),
            pltpu.VMEM((mem_length, local), f32),
        ],
        flops=1.6e10,
        moved=2e7,
    )
    send_qb, d_b, send_m = rest_b[:4], rest_b[4], rest_b[5:]
    recv_qb = exchange(send_qb[1:])
    grad_first, grad_first_low, gain_grad_b = run(
        cross_norm_back_kernel, [index],
        [send_qb[0], *recv_qb, attention_w, first_h, gain_cross, grad_second],
        [shape((rows, width), f32), shape((rows, width), bf16), shape((1, width), f32)],
        flops=4e8, moved=5e6, blocks={4: ((4, local, width), (0, 3, 0))},
    )
    parts_ga = gather_parts(grad_first_low)

    cross_grads = rows_sum_halves(
        jnp.concatenate(
            [plain(dq_b, whole_b), weight_grad(d_b, memory_all), plain(o_b, whole_gc)], axis=0
        ),
    )

    share = lax.dot_general(
        after(hidden, parts_gc[3]), ffn_down, (((1,), (0,)), ((), ())),
        preferred_element_type=f32,
    ).reshape(4, rows, width)
    out1 = swap(share[1].astype(bf16), 1)
    out3 = swap(share[3].astype(bf16), 1)
    out2 = swap((share[2] + out3.astype(f32)).astype(bf16), 2)
    layer_out = (second_h + (share[0] + out1.astype(f32)) + out2.astype(f32)).astype(bf16)

    recv_m = exchange([after(piece, parts_ga[3]) for piece in send_m[1:]])
    grad_memory = memory_grads(index, [send_m[0], *recv_m], memory_w)

    (whole_ga, d_a, *rest_a) = run(
        functools.partial(self_backward_kernel, heads),
        [index],
        [starts, bias, *parts_ga, self_out, q_a, k_a, v_a, kt_a, ot_a, lse_a],
        [shape((length, width), bf16), shape((3 * local, length), bf16)]
        + [shape((3, local, rows), bf16)] * 4
        + [shape((WIDE, heads * QB), f32)],
        [
            pltpu.VMEM((heads, length, local), bf16),
            pltpu.VMEM((local, length), f32),
            pltpu.VMEM((local, length), bf16),
            pltpu.VMEM((BAND + length, local), f32),
            pltpu.VMEM((BAND + length, local), f32),
        ],
        flops=8e9,
        moved=1e7,
    )
    send_pa, bias_sum = rest_a[:4], rest_a[4]
    self_grads = rows_sum_halves(
        jnp.concatenate([plain(d_a, whole_a), plain(o_a, whole_ga)], axis=0)
    )

    recv_pa = exchange(send_pa[1:])
    grad_input, gain_grad_a = run(
        self_norm_back_kernel, [index],
        [send_pa[0], *recv_pa, attention_w, hidden_2d, gain_self, grad_first],
        [shape((rows, 1, width), f32), shape((1, width), f32)],
        flops=1.2e9, moved=8e6, blocks={4: ((4, 3 * local, width), (0, 0, 0))},
    )

    (bias_parts,) = run(
        functools.partial(bias_grad_kernel, heads), [], [bias_sum],
        [shape((heads, len(bucket_starts), QB), f32)], flops=1e7, moved=6e5,
    )
    grad_table = jnp.sum(bias_parts, axis=2).T

    gains = total_over(jnp.concatenate([gain_grad_a, gain_grad_b, gain_grad_c], axis=0), "narrow")
    small = total_over(
        jnp.concatenate([gains.reshape(-1), grad_table.reshape(-1)]), "rows"
    )
    gain_totals = small[: 3 * width].reshape(3, width)
    table_total = small[3 * width :].reshape(grad_table.shape)

    def finished(total):
        columns = [total[n * local : (n + 1) * local].astype(f32).T for n in range(3)]
        return columns + [total[3 * local :].astype(f32)]

    cross_done = finished(cross_grads)
    self_done = finished(self_grads)

    return (
        layer_out.reshape(rows, 1, width),
        grad_input,
        grad_memory,
        gain_totals[0],
        gain_totals[1],
        gain_totals[2],
        table_total,
        *self_done,
        *cross_done,
        ffn_grads[0],
        ffn_grads[1],
        ffn_grads[2],
    )


def solution(mesh):
    in_specs = (
        P("narrow", "rows", None),
        P("narrow", "rows", None),
        P("narrow", "rows", None),
        P("rows", None),
        P("rows", None),
        P(),
        P(),
        P(),
        P(None, "narrow"),
        P(None, "narrow"),
        P(None, "narrow"),
        P(None, "narrow"),
        P("narrow", None),
        P(None, "narrow"),
        P(None, "narrow"),
        P(None, "narrow"),
        P("narrow", None),
        P(None, "narrow"),
        P(None, "narrow"),
        P("narrow", None),
    )
    out_specs = (
        P("narrow", "rows", None),
        P("narrow", "rows", None),
        P("narrow", "rows", None),
        P(),
        P(),
        P(),
        P(None, "narrow"),
        P(None, "narrow"),
        P(None, "narrow"),
        P(None, "narrow"),
        P("narrow", None),
        P(None, "narrow"),
        P(None, "narrow"),
        P(None, "narrow"),
        P("narrow", None),
        P(None, "narrow"),
        P(None, "narrow"),
        P("narrow", None),
    )

    return jax.shard_map(body, mesh=mesh, in_specs=in_specs, out_specs=out_specs, check_vma=False)
```
